512 devices in a mesh: cls: 16 (over x, y), pose: 32 (over z, core).
Axes of the slice: x: 4, y: 4, z: 16, core: 2. Of those that a mesh axis runs over, the one named last changes fastest.
Arguments:
- images: bfloat16 [512, 16384], P(('pose', 'cls')), may hold values from -6 to 6
- significant: int32 [512, 3], P(('pose', 'cls')), may hold values from 0 to 31, all different within a row; in each aligned block of 16 rows (0 to 15, 16 to 31, ...) at most 3 rows name the same one
- projections: bfloat16 [32, 512, 16384], P('cls', 'pose')
- phase: float32 [4, 8192], replicated, may hold values from -3.140625 to 3.140625
Outputs:
- back_sums: bfloat16 [32, 512, 16384], P('cls', 'pose')
- evidence: float32 [512], P(('pose', 'cls'))
The draws below stay inside these ranges and needn't reach their ends.
Inputs may be any that keep to these rules, and one draw needn't show every extreme that they name: `significant`: each particle names 3 different bins. Of the particles of one aligned block of 16 rows, at most 3 name one bin.
All inputs are finite; a program needn't handle non-finite values.
Results may differ from the reference program's by a relative error of at most 0.012.
The reference program's roundings to bfloat16 on the way (of `shifted` and `weight`) count: a program that leaves them out, or rounds other values in their place, can miss the bound.
Values may be sent and summed in bfloat16 or wider, within the bound.
No kernel may reach another device: no remote copies, remote signals or barrier semaphores. Data moves between devices by JAX's collectives and lax.ppermute only.
A program may use at most 64 MiB of HBM per device.

```python
import math
import jax
import jax.numpy as jnp
import numpy as np
from jax import lax

COEF = 8192
KS = 3
NT = 4
PPD = 16
CLASSES = 32
BINS = 32
POSES = 512
GR = 16
PART = 512
CAP = 3


def draw_projections(key, part):
    shape = (CLASSES, POSES, 2 * COEF)
    base_scale = (2.0 * COEF) ** (-0.5)
    key_main = jax.random.fold_in(key, 11)
    values = jnp.clip(jax.random.normal(key_main, shape, jnp.float32), -6.0, 6.0)
    return (values * base_scale).astype(jnp.bfloat16)


def block_levels(stream_key, shape, shards, low, top_value):
    gain = 1.0
    for position, parts in shards:
        steps = jax.random.uniform(jax.random.fold_in(jax.random.fold_in(stream_key, 6), position), (parts,), jnp.float32, low / len(shards), top_value / len(shards))
        gain = gain * jnp.repeat(jnp.exp(steps), shape[position] // parts).reshape((-1,) + (1,) * (len(shape) - 1 - position))
    return gain


def assign_block(stream_key, own, number, rows, amount, top, reach, lean):
    order = jax.random.permutation(stream_key, amount)
    packed, ordinary = load_shares(amount, rows * top, reach, lean, True), load_shares(amount, rows * top, reach, lean, False)
    places = jnp.arange(amount)

    def named(sizes, offset_by):
        used = int((sizes > 0).sum())
        fixed = max(1, used // 4)
        passed = fixed + (places - fixed + offset_by * (used - fixed)) % max(1, amount - fixed)
        return jnp.zeros((amount,), jnp.int32).at[order[jnp.where(places < fixed, places, passed)]].set(jnp.asarray(sizes, jnp.int32))

    sizes = jnp.where(number % 4 == 0, named(packed, number // 4), named(ordinary, number - number // 4 - 1))
    mixed = jax.random.permutation(jax.random.fold_in(own, 3), amount)
    giver, sink = mixed[0:amount // 2 * 2:2], mixed[1:amount // 2 * 2:2]
    margin = jnp.minimum(sizes[giver] - 1, reach - sizes[sink]) // 2
    margin = jnp.where((giver == order[0]) | (sink == order[0]) | (sizes[sink] == 0), 0, jnp.maximum(margin, 0))
    passed = jax.random.randint(jax.random.fold_in(own, 4), (amount // 2,), 0, 1 << 20) % (margin + 1)
    sizes = sizes.at[giver].add(-passed).at[sink].add(passed)
    members = jnp.searchsorted(jnp.cumsum(sizes), jnp.arange(rows * top), side="right").astype(jnp.int32)
    table = members.reshape(top, rows).T
    table = table[jax.random.permutation(jax.random.fold_in(own, 1), rows)]
    offset_by = jax.random.randint(jax.random.fold_in(own, 2), (rows, 1), 0, top)
    return jnp.take_along_axis(table, (jnp.arange(top)[None, :] + offset_by) % top, axis=1)


def load_shares(number_of, total, most, slope, full):
    loads = [(1 << 20) // math.isqrt(standing ** slope) + 1 for standing in range(1, number_of + 1)]
    largest = most if full else min(most, max(-(-total // number_of), total * loads[0] // sum(loads)))
    least = 1 if total - largest >= number_of - 1 else 0
    given, surplus = [largest] + [least] * (number_of - 1), total - largest - least * (number_of - 1)
    while surplus > 0:
        movable = [i for i in range(1, number_of) if given[i] < largest] or [i for i in range(1, number_of) if given[i] < most]
        mass, left = sum([loads[i] for i in movable]), surplus
        for i in movable:
            addition = min(most - given[i], max(1, left * loads[i] // mass), surplus)
            given[i] = given[i] + addition
            surplus = surplus - addition
    return np.array(given)


def gaussian(rng, extent, spread, bound, pieces=(), held_as=jnp.bfloat16):
    drawn = spread * jax.random.normal(rng, extent, jnp.float32)
    if pieces:
        drawn = drawn * block_levels(rng, extent, pieces, -0.22, 0.18)
    return jnp.clip(drawn, -bound, bound).astype(held_as)


def setup_inputs(seed: int = 0) -> dict:
    arg_keys = jax.random.split(jax.random.key(seed), 5)
    images = gaussian(arg_keys[0], (PART, 2 * COEF), 1.0, 6.0, ((0, 512),))
    significant_keys = jax.random.split(jax.random.fold_in(arg_keys[1], 1), PART // GR)
    significant_turns = jax.random.permutation(jax.random.fold_in(arg_keys[1], 3), PART // GR)
    significant = jax.vmap(lambda own, number: assign_block(jax.random.fold_in(arg_keys[1], 2), own, number, GR, BINS, KS, CAP, 2))(significant_keys, significant_turns).reshape((PART, KS))
    projections = draw_projections(jax.random.fold_in(arg_keys[4], 71), 0)
    phase = jnp.clip(jax.random.uniform(arg_keys[3], (NT, COEF), jnp.float32, -3.140625, 3.140625), -3.140625, 3.140625)
    return {"images": images, "significant": significant, "projections": projections, "phase": phase}


def rotate(block, cosv, sinv):
    real = block[:, :COEF]
    imag = block[:, COEF:]
    return jnp.concatenate([cosv * real - sinv * imag, sinv * real + cosv * imag], axis=1)


def unrotate(block, cosv, sinv):
    real = block[:, :COEF]
    imag = block[:, COEF:]
    return jnp.concatenate([cosv * real + sinv * imag, cosv * imag - sinv * real], axis=1)


def reference(images, significant, projections, phase):
    most_rows = BINS * CAP
    width = 2 * COEF
    cosv = jnp.cos(phase.astype(jnp.float32))
    sinv = jnp.sin(phase.astype(jnp.float32))
    proj_bins = projections.reshape(CLASSES, BINS, PPD, width)

    def per_bin(index):
        member = jnp.any(significant == index, axis=1)
        order = jnp.argsort(1 - member.astype(jnp.int32), stable=True)[:most_rows].astype(jnp.int32)
        valid = member[order]
        rows = jnp.where(valid[:, None], images[order], jnp.zeros((), images.dtype))
        rows_wide = rows.astype(jnp.float32)
        block = lax.dynamic_index_in_dim(proj_bins, index, 1, keepdims=False)
        block = block.reshape(CLASSES * PPD, width).astype(jnp.float32)
        scores = []
        for step in range(NT):
            shifted = rotate(block, cosv[step], sinv[step]).astype(jnp.bfloat16)
            shifted = lax.optimization_barrier(shifted).astype(jnp.float32)
            scores.append(jnp.dot(rows_wide, shifted.T, precision=lax.Precision.HIGHEST))
        return order, valid, rows, jnp.stack(scores, 0)

    order, valid, rows, scores = lax.map(per_bin, jnp.arange(BINS, dtype=jnp.int32))
    segment = jnp.where(valid, order, PART).reshape(-1)
    row_top = jnp.max(scores, axis=(1, 3)).reshape(-1)
    top = jax.ops.segment_max(row_top, segment, num_segments=PART + 1)[:PART]
    row_ref = jnp.take(top, order.reshape(-1)).reshape(BINS, 1, most_rows, 1)
    row_sum = jnp.sum(jnp.exp(scores - row_ref), axis=(1, 3)).reshape(-1)
    total = jax.ops.segment_sum(row_sum, segment, num_segments=PART + 1)[:PART]
    evidence = top + jnp.log(total)

    def back_bin(items):
        bin_order, bin_rows, bin_scores = items
        level = jnp.take(evidence, bin_order)
        rows_wide = bin_rows.astype(jnp.float32)
        accum = jnp.zeros((CLASSES * PPD, width), jnp.float32)
        for step in range(NT):
            weight = jnp.exp(bin_scores[step] - level[:, None]).astype(jnp.bfloat16)
            weight = lax.optimization_barrier(weight).astype(jnp.float32)
            partial_sum = jnp.dot(weight.T, rows_wide, precision=lax.Precision.HIGHEST)
            accum = accum + unrotate(partial_sum, cosv[step], sinv[step])
        return accum.astype(jnp.bfloat16).reshape(CLASSES, PPD, width)

    backs = lax.map(back_bin, (order, rows, scores))
    back_sums = jnp.transpose(backs, (1, 0, 2, 3)).reshape(CLASSES, POSES, width)
    return back_sums, evidence
```

```python
import jax
import jax.numpy as jnp
from jax import lax
from jax.experimental import pallas as pl
from jax.experimental.pallas import tpu as pltpu
from jax.sharding import Mesh, PartitionSpec as P

BF = jnp.bfloat16
F32 = jnp.float32
I32 = jnp.int32
NEG = -3.0e38

NX, NY, NZ, NC = 4, 4, 16, 2
NG = NX * NY
GR = 16
CAP = 3
BINS = 32
NT = 4
COEF = 8192
CH = COEF // NG
CW = 2 * CH
PAIR = 32
COMB = NT * PAIR
SLOTS = 2 * GR * CAP


def iota(shape, dim):
    return lax.broadcasted_iota(I32, shape, dim)


def nt_dot(a, b):
    return lax.dot_general(a, b, (((1,), (1,)), ((), ())), preferred_element_type=F32)


def nn_dot(a, b):
    return lax.dot_general(a, b, (((1,), (0,)), ((), ())), preferred_element_type=F32)


def vmem():
    return pl.BlockSpec(memory_space=pltpu.VMEM)


def smem():
    return pl.BlockSpec(memory_space=pltpu.SMEM)


def select_kernel(idx_ref, x_ref, out_ref, own_ref, scr):
    core = idx_ref[0]
    scr[...] = x_ref[...].astype(F32).reshape(2 * GR * 16, 128)
    member = scr[pl.ds(8, 2 * GR, stride=16), :]
    row = iota((32, 32), 0)
    col = iota((32, 32), 1)
    tri = jnp.where((row // GR == col // GR) & (col < row), 1.0, 0.0).astype(BF)
    rank = nn_dot(tri, member.astype(BF))
    both = (member + pltpu.roll(rank, 32, 1)).astype(BF)
    pick = (iota((128, 128), 1) == 2 * (iota((128, 128), 0) // 8) + core).astype(F32).astype(BF)
    mem = nt_dot(pick, member.astype(BF))
    rnk = nt_dot(pick, rank.astype(BF)).astype(I32)
    k = iota((128, 32), 0) % 8
    block = iota((128, 32), 1) // GR
    rnk = jnp.where(mem > 0.5, rnk + CAP * block, -1)
    rank_ok = (rnk >= CAP * block) & (rnk < CAP * block + CAP)
    rnk = jnp.where(rank_ok, rnk, -1)
    sel = jnp.where(rnk == k, 1.0, 0.0).astype(BF)
    for j in range(8):
        rows = scr[pl.ds(j, 2 * GR, stride=16), :].astype(BF)
        o = nn_dot(sel, rows)
        if j < 6:
            sel6 = jnp.where((k == 6) & (rnk == j), 1.0, 0.0).astype(BF)
            o = o + nn_dot(sel6, both)
        out_ref[:, j * 128 : (j + 1) * 128] = o.astype(BF)
    mine = iota((32, 128), 0) == core * GR + idx_ref[2]
    own = jnp.sum(jnp.where(mine, both.astype(F32), 0.0), axis=0, keepdims=True)
    own_ref[...] = jnp.broadcast_to(own, (8, 128))


def spread_kernel(y_ref, out_ref, scr, sem):
    s = iota((SLOTS, 128), 0)
    compact = jnp.where(iota((SLOTS, 128), 1) == (s // 6) * 8 + s % 6, 1.0, 0.0).astype(BF)
    scr[...] = nn_dot(compact, y_ref[...]).astype(BF)
    copies = [pltpu.make_async_copy(scr, out_ref.at[g], sem.at[g]) for g in range(NG)]
    for c in copies:
        c.start()
    for c in copies:
        c.wait()


def info_kernel(idx_ref, y_ref, own_ref, out_ref):
    s = iota((128, 128), 0)
    info = jnp.zeros((128, 128), F32)
    for j in range(6):
        hit = (iota((128, 128), 1) == (s // 6) * 8 + 6) & (s % 6 == j) & (s < SLOTS)
        info = info + nn_dot(
            jnp.where(hit, 1.0, 0.0).astype(BF), y_ref[:, j * 128 : (j + 1) * 128]
        )
    info = info.astype(BF)
    own = own_ref[...].astype(BF)
    z = iota((16, 128), 0)
    lane = iota((16, 128), 1)
    for c in range(2):
        pm = jnp.where(lane == 2 * z + c, 1.0, 0.0).astype(BF)
        pr = jnp.where(lane == 32 + 2 * z + c, 1.0, 0.0).astype(BF)
        out_ref[c] = nt_dot(pm, info)
        out_ref[2 + c] = nt_dot(pr, info)
        om = nt_dot(pm, own)[:, :1]
        orank = nt_dot(pr, own)[:, :1].astype(I32)
        out_ref[4 + c] = jnp.where((om > 0.5) & (lane == CAP * idx_ref[1] + orank), 1.0, 0.0)


def rotate_kernel(p_ref, c_ref, s_ref, out_ref):
    pr = p_ref[0].astype(F32)
    pi = p_ref[1].astype(F32)
    for t in range(NT):
        c = c_ref[t : t + 1, :]
        s = s_ref[t : t + 1, :]
        out_ref[0, t * PAIR : (t + 1) * PAIR, :CH] = (c * pr - s * pi).astype(BF)
        out_ref[0, t * PAIR : (t + 1) * PAIR, CH:] = (s * pr + c * pi).astype(BF)


def score_kernel(t_ref, r_ref, score_ref, lse_ref):
    acc = nt_dot(t_ref[0], r_ref[0])
    for g in range(1, NG):
        acc = acc + nt_dot(t_ref[g], r_ref[g])
    score_ref[...] = jnp.zeros((COMB, 128), F32)
    score_ref[:, :SLOTS] = acc
    sc = score_ref[...]
    top = jnp.max(sc, axis=0, keepdims=True)
    lse = top + jnp.log(jnp.sum(jnp.exp(sc - top), axis=0, keepdims=True))
    lse_ref[...] = jnp.broadcast_to(lse[None], (NC * NG, 1, 128))


def merge_kernel(l_ref, out_ref):
    parts = []
    for c in range(NC):
        v = l_ref[c * NG : (c + 1) * NG].reshape(NG, 128)
        top = jnp.max(v, axis=0, keepdims=True)
        parts.append(top + jnp.log(jnp.sum(jnp.exp(v - top), axis=0, keepdims=True)))
    both = jnp.concatenate(parts, axis=0)
    out_ref[...] = jnp.broadcast_to(both[None], (NZ, NC, 128))


def back_kernel(l_ref, info_ref, score_ref, r_ref, c_ref, s_ref, out_ref, ev_ref):
    lane3 = iota((NZ, 128), 1) % CAP
    sel, own = [], []
    for c in range(NC):
        level = l_ref[:, c, :]
        shift = info_ref[2 + c].astype(I32) - lane3
        v = level
        for d in (-2, -1, 1, 2):
            v = jnp.where(shift == d, pltpu.roll(level, (-d) % 128, 1), v)
        sel.append(jnp.where(info_ref[c] > 0.5, v, NEG))
        own.append(jnp.where(info_ref[4 + c] > 0.5, level, NEG))

    def lse(pair, axes):
        top = jnp.max(jnp.maximum(pair[0], pair[1]), axis=axes, keepdims=True)
        tot = sum(jnp.where(v > 0.5 * NEG, jnp.exp(v - top), 0.0) for v in pair)
        return top, jnp.sum(tot, axis=axes, keepdims=True)

    top, tot = lse(own, (0, 1))
    ev_ref[...] = jnp.broadcast_to(top + jnp.log(tot), (8, 128))
    top, tot = lse(sel, (0,))
    level = jnp.where(tot > 0.0, top + jnp.log(jnp.where(tot > 0.0, tot, 1.0)), 0.0)
    w = jnp.exp(score_ref[...] - level)[:, :SLOTS].astype(BF)
    for g in range(NG):
        part = nn_dot(w, r_ref[g])
        re = jnp.zeros((PAIR, CH), F32)
        im = jnp.zeros((PAIR, CH), F32)
        for t in range(NT):
            c = c_ref[t : t + 1, g * CH : (g + 1) * CH]
            s = s_ref[t : t + 1, g * CH : (g + 1) * CH]
            gr = part[t * PAIR : (t + 1) * PAIR, :CH]
            gi = part[t * PAIR : (t + 1) * PAIR, CH:]
            re = re + (c * gr + s * gi)
            im = im + (c * gi - s * gr)
        out_ref[:, g * CH : (g + 1) * CH] = re.astype(BF)
        out_ref[:, COEF + g * CH : COEF + (g + 1) * CH] = im.astype(BF)


def a2a(v, axes):
    return lax.all_to_all(v, axes, split_axis=0, concat_axis=0, tiled=True)


def per_device(images, significant, projections, phase):
    core = lax.axis_index("core")
    pose = lax.axis_index(("z", "core"))
    group = lax.axis_index(("x", "y"))
    idx = jnp.stack([core, pose, group]).astype(I32)

    chunks = images.reshape(2, NG, CH // 128, 128).transpose(1, 0, 2, 3).reshape(NG, 8, 128)
    lanes = jnp.arange(128, dtype=I32)
    member = jnp.any(significant.reshape(-1, 1) == lanes[None, :], axis=0).astype(BF)
    extra = jnp.where(jnp.arange(8)[:, None] == 0, member[None, :], jnp.zeros((), BF))
    first = jnp.concatenate([chunks, jnp.broadcast_to(extra[None], (NG, 8, 128))], axis=1)
    first = jnp.concatenate([first, first], axis=0)
    x1 = a2a(first, ("core", "x", "y"))

    cosv = jnp.cos(phase)
    sinv = jnp.sin(phase)
    proj = projections.reshape(PAIR, 2, COEF).transpose(1, 0, 2)
    table = pl.pallas_call(
        rotate_kernel,
        grid=(NG,),
        in_specs=[
            pl.BlockSpec((2, PAIR, CH), lambda g: (0, 0, g)),
            pl.BlockSpec((NT, CH), lambda g: (0, g)),
            pl.BlockSpec((NT, CH), lambda g: (0, g)),
        ],
        out_specs=pl.BlockSpec((1, COMB, CW), lambda g: (g, 0, 0)),
        out_shape=jax.ShapeDtypeStruct((NG, COMB, CW), BF),
        name="rotate",
    )(proj, cosv, sinv)

    picked, own = pl.pallas_call(
        select_kernel,
        in_specs=[smem(), vmem()],
        out_specs=[vmem(), vmem()],
        out_shape=[
            jax.ShapeDtypeStruct((NZ * 8, CW), BF),
            jax.ShapeDtypeStruct((8, 128), F32),
        ],
        scratch_shapes=[pltpu.VMEM((2 * GR * 16, 128), F32)],
        name="select",
    )(idx, x1)
    y2 = a2a(picked.reshape(NZ, 8, CW), "z").reshape(NZ * 8, CW)

    spread = pl.pallas_call(
        spread_kernel,
        in_specs=[vmem()],
        out_specs=pl.BlockSpec(memory_space=pl.ANY),
        out_shape=jax.ShapeDtypeStruct((NG, SLOTS, CW), BF),
        scratch_shapes=[pltpu.VMEM((SLOTS, CW), BF), pltpu.SemaphoreType.DMA((NG,))],
        name="spread",
    )(y2)
    rows = a2a(spread, ("x", "y"))
    info = pl.pallas_call(
        info_kernel,
        in_specs=[smem(), vmem(), vmem()],
        out_specs=vmem(),
        out_shape=jax.ShapeDtypeStruct((6, NZ, 128), F32),
        name="info",
    )(idx, y2, own)

    scores, lse = pl.pallas_call(
        score_kernel,
        in_specs=[vmem(), vmem()],
        out_specs=[vmem(), vmem()],
        out_shape=[
            jax.ShapeDtypeStruct((COMB, 128), F32),
            jax.ShapeDtypeStruct((NC * NG, 1, 128), F32),
        ],
        name="score",
    )(table, rows)
    l4 = a2a(lse, ("core", "x", "y"))
    merged = pl.pallas_call(
        merge_kernel,
        in_specs=[vmem()],
        out_specs=vmem(),
        out_shape=jax.ShapeDtypeStruct((NZ, NC, 128), F32),
        name="merge",
    )(l4)
    l5 = a2a(merged, "z")

    back, ev = pl.pallas_call(
        back_kernel,
        in_specs=[vmem()] * 6,
        out_specs=[vmem(), vmem()],
        out_shape=[
            jax.ShapeDtypeStruct((PAIR, 2 * COEF), BF),
            jax.ShapeDtypeStruct((8, 128), F32),
        ],
        name="back",
    )(l5, info, scores, rows, cosv, sinv)
    return back.reshape(projections.shape), ev[0, :1]


def solution(mesh):
    fine = Mesh(mesh.devices.reshape(NX, NY, NZ, NC), ("x", "y", "z", "core"))
    every = ("z", "core", "x", "y")
    cls = ("x", "y")
    pose = ("z", "core")
    return jax.shard_map(
        per_device,
        mesh=fine,
        in_specs=(P(every, None), P(every, None), P(cls, pose, None), P()),
        out_specs=(P(cls, pose, None), P(every)),
        check_vma=False,
    )
```

```python
import jax
import jax.numpy as jnp
from jax import lax
from jax.experimental import pallas as pl
from jax.experimental.pallas import tpu as pltpu
from jax.sharding import Mesh, PartitionSpec as P

BF = jnp.bfloat16
F32 = jnp.float32
I32 = jnp.int32
NEG = -3.0e38

NX, NY, NZ, NC = 4, 4, 16, 2
NG = NX * NY
GR = 16
CAP = 3
BINS = 32
NT = 4
COEF = 8192
CH = COEF // NG
CW = 2 * CH
PAIR = 32
COMB = NT * PAIR
SLOTS = 2 * GR * CAP


def iota(shape, dim):
    return lax.broadcasted_iota(I32, shape, dim)


def nt_dot(a, b):
    return lax.dot_general(a, b, (((1,), (1,)), ((), ())), preferred_element_type=F32)


def nn_dot(a, b):
    return lax.dot_general(a, b, (((1,), (0,)), ((), ())), preferred_element_type=F32)


def vmem():
    return pl.BlockSpec(memory_space=pltpu.VMEM)


def anywhere():
    return pl.BlockSpec(memory_space=pltpu.HBM)


def smem():
    return pl.BlockSpec(memory_space=pltpu.SMEM)


def prepare_kernel(sig_ref, x_ref, out_ref, scr):
    lane = iota((1, 128), 1)
    hit = (lane == sig_ref[0, 0]) | (lane == sig_ref[0, 1]) | (lane == sig_ref[0, 2])
    member = jnp.where(hit, 1.0, 0.0)
    scr[...] = jnp.zeros((NG * 16, 128), F32)
    scr[pl.ds(8, NG, stride=16), :] = jnp.broadcast_to(member, (NG, 128))
    x = x_ref[...].astype(F32)
    for g in range(NG):
        for j in range(CH // 128):
            at = g * CH + j * 128
            scr[g * 16 + j : g * 16 + j + 1, :] = x[:, at : at + 128]
            at = at + COEF
            scr[g * 16 + 4 + j : g * 16 + 5 + j, :] = x[:, at : at + 128]
    v = scr[...].reshape(NG, 16, 128).astype(BF)
    out_ref[:NG] = v
    out_ref[NG:] = v


def select_kernel(idx_ref, x_ref, out_ref, own_ref, scr):
    core = idx_ref[0]
    scr[...] = x_ref[...].astype(F32).reshape(2 * GR * 16, 128)
    member = scr[pl.ds(8, 2 * GR, stride=16), :]
    row = iota((32, 32), 0)
    col = iota((32, 32), 1)
    tri = jnp.where((row // GR == col // GR) & (col < row), 1.0, 0.0).astype(BF)
    rank = nn_dot(tri, member.astype(BF))
    both = (member + pltpu.roll(rank, 32, 1)).astype(BF)
    pick = (iota((128, 128), 1) == 2 * (iota((128, 128), 0) // 8) + core).astype(F32).astype(BF)
    mem = nt_dot(pick, member.astype(BF))
    rnk = nt_dot(pick, rank.astype(BF)).astype(I32)
    k = iota((128, 32), 0) % 8
    block = iota((128, 32), 1) // GR
    rnk = jnp.where(mem > 0.5, rnk + CAP * block, -1)
    rank_ok = (rnk >= CAP * block) & (rnk < CAP * block + CAP)
    rnk = jnp.where(rank_ok, rnk, -1)
    sel = jnp.where(rnk == k, 1.0, 0.0).astype(BF)
    for j in range(8):
        rows = scr[pl.ds(j, 2 * GR, stride=16), :].astype(BF)
        o = nn_dot(sel, rows)
        if j < 6:
            sel6 = jnp.where((k == 6) & (rnk == j), 1.0, 0.0).astype(BF)
            o = o + nn_dot(sel6, both)
        out_ref[:, j * 128 : (j + 1) * 128] = o.astype(BF)
    mine = iota((32, 128), 0) == core * GR + idx_ref[2]
    own = jnp.sum(jnp.where(mine, both.astype(F32), 0.0), axis=0, keepdims=True)
    own_ref[...] = jnp.broadcast_to(own, (8, 128))


def spread_kernel(y_ref, out_ref, scr, sem):
    s = iota((SLOTS, 128), 0)
    compact = jnp.where(iota((SLOTS, 128), 1) == (s // 6) * 8 + s % 6, 1.0, 0.0).astype(BF)
    scr[...] = nn_dot(compact, y_ref[...]).astype(BF)
    copies = [pltpu.make_async_copy(scr, out_ref.at[g], sem.at[g]) for g in range(NG)]
    for c in copies:
        c.start()
    for c in copies:
        c.wait()


def info_kernel(idx_ref, y_ref, own_ref, out_ref):
    s = iota((128, 128), 0)
    info = jnp.zeros((128, 128), F32)
    for j in range(6):
        hit = (iota((128, 128), 1) == (s // 6) * 8 + 6) & (s % 6 == j) & (s < SLOTS)
        info = info + nn_dot(
            jnp.where(hit, 1.0, 0.0).astype(BF), y_ref[:, j * 128 : (j + 1) * 128]
        )
    info = info.astype(BF)
    own = own_ref[...].astype(BF)
    z = iota((16, 128), 0)
    lane = iota((16, 128), 1)
    for c in range(2):
        pm = jnp.where(lane == 2 * z + c, 1.0, 0.0).astype(BF)
        pr = jnp.where(lane == 32 + 2 * z + c, 1.0, 0.0).astype(BF)
        out_ref[c] = nt_dot(pm, info)
        out_ref[2 + c] = nt_dot(pr, info)
        om = nt_dot(pm, own)[:, :1]
        orank = nt_dot(pr, own)[:, :1].astype(I32)
        out_ref[4 + c] = jnp.where((om > 0.5) & (lane == CAP * idx_ref[1] + orank), 1.0, 0.0)


def rotate_kernel(p_ref, c_ref, s_ref, out_ref):
    for g in range(NG):
        lo = g * CH
        pr = p_ref[:, lo : lo + CH].astype(F32)
        pi = p_ref[:, COEF + lo : COEF + lo + CH].astype(F32)
        for t in range(NT):
            c = c_ref[t : t + 1, lo : lo + CH]
            s = s_ref[t : t + 1, lo : lo + CH]
            out_ref[g, t * PAIR : (t + 1) * PAIR, :CH] = (c * pr - s * pi).astype(BF)
            out_ref[g, t * PAIR : (t + 1) * PAIR, CH:] = (s * pr + c * pi).astype(BF)


def score_kernel(t_ref, r_ref, score_ref, lse_ref, scr, sem):
    copies = [pltpu.make_async_copy(t_ref.at[g], scr.at[g], sem.at[g]) for g in range(NG)]
    for c in copies:
        c.start()
    acc = jnp.zeros((COMB, SLOTS), F32)
    for g in range(NG):
        copies[g].wait()
        acc = acc + nt_dot(scr[g], r_ref[g])
    score_ref[...] = jnp.zeros((COMB, 128), F32)
    score_ref[:, :SLOTS] = acc
    sc = score_ref[...]
    top = jnp.max(sc, axis=0, keepdims=True)
    lse = top + jnp.log(jnp.sum(jnp.exp(sc - top), axis=0, keepdims=True))
    lse_ref[...] = jnp.broadcast_to(lse[None], (NC * NG, 1, 128))


def merge_kernel(l_ref, out_ref):
    parts = []
    for c in range(NC):
        v = l_ref[c * NG : (c + 1) * NG].reshape(NG, 128)
        top = jnp.max(v, axis=0, keepdims=True)
        parts.append(top + jnp.log(jnp.sum(jnp.exp(v - top), axis=0, keepdims=True)))
    both = jnp.concatenate(parts, axis=0)
    out_ref[...] = jnp.broadcast_to(both[None], (NZ, NC, 128))


def back_kernel(
    l_ref, info_ref, score_ref, r_ref, cos_ref, sin_ref, out_ref, ev_ref, c_ref, s_ref, sem
):
    copies = [
        pltpu.make_async_copy(cos_ref, c_ref, sem.at[0]),
        pltpu.make_async_copy(sin_ref, s_ref, sem.at[1]),
    ]
    for c in copies:
        c.start()
    lane3 = iota((NZ, 128), 1) % CAP
    sel, own = [], []
    for c in range(NC):
        level = l_ref[:, c, :]
        shift = info_ref[2 + c].astype(I32) - lane3
        v = level
        for d in (-2, -1, 1, 2):
            v = jnp.where(shift == d, pltpu.roll(level, (-d) % 128, 1), v)
        sel.append((info_ref[c] > 0.5, v))
        own.append((info_ref[4 + c] > 0.5, level))

    def lse(pair, axes):
        a, b = (jnp.where(m, v, NEG) for m, v in pair)
        top = jnp.max(jnp.maximum(a, b), axis=axes, keepdims=True)
        tot = sum(jnp.where(m, jnp.exp(v - top), 0.0) for m, v in pair)
        return top, jnp.sum(tot, axis=axes, keepdims=True)

    top, tot = lse(own, (0, 1))
    ev_ref[...] = top + jnp.log(tot)
    top, tot = lse(sel, (0,))
    level = jnp.where(tot > 0.0, top + jnp.log(jnp.where(tot > 0.0, tot, 1.0)), 0.0)
    w = jnp.exp(score_ref[...] - level)[:, :SLOTS].astype(BF)
    for c in copies:
        c.wait()
    for g in range(NG):
        part = nn_dot(w, r_ref[g])
        re = jnp.zeros((PAIR, CH), F32)
        im = jnp.zeros((PAIR, CH), F32)
        for t in range(NT):
            c = c_ref[t : t + 1, g * CH : (g + 1) * CH]
            s = s_ref[t : t + 1, g * CH : (g + 1) * CH]
            gr = part[t * PAIR : (t + 1) * PAIR, :CH]
            gi = part[t * PAIR : (t + 1) * PAIR, CH:]
            re = re + (c * gr + s * gi)
            im = im + (c * gi - s * gr)
        out_ref[:, g * CH : (g + 1) * CH] = re.astype(BF)
        out_ref[:, COEF + g * CH : COEF + (g + 1) * CH] = im.astype(BF)


def a2a(v, axes):
    return lax.all_to_all(v, axes, split_axis=0, concat_axis=0, tiled=True)


def call(kernel, name, operands, outs, near=(), far=(), away=(), scalars=0, scratch=()):
    operands = [
        pltpu.with_memory_space_constraint(v, pltpu.VMEM if n in near else pltpu.HBM)
        if n in near or n in far
        else v
        for n, v in enumerate(operands)
    ]
    return pl.pallas_call(
        kernel,
        in_specs=[
            smem() if n < scalars else anywhere() if n in far else vmem()
            for n in range(len(operands))
        ],
        out_specs=[anywhere() if n in away else vmem() for n in range(len(outs))],
        out_shape=list(outs),
        scratch_shapes=scratch,
        compiler_params=pltpu.CompilerParams(vmem_limit_bytes=16 << 20),
        name=name,
    )(*operands)


def per_device(images, significant, projections, phase):
    core = lax.axis_index("core")
    pose = lax.axis_index(("z", "core"))
    group = lax.axis_index(("x", "y"))
    idx = jnp.stack([core, pose, group]).astype(I32)

    (first,) = call(
        prepare_kernel,
        "prepare",
        [significant, images],
        [pltpu.VMEM((NC * NG, 16, 128), BF)],
        scalars=1,
        scratch=[pltpu.VMEM((NG * 16, 128), F32)],
    )
    x1 = a2a(first, ("core", "x", "y"))

    cosv = jnp.cos(phase)
    sinv = jnp.sin(phase)
    (table,) = call(
        rotate_kernel,
        "rotate",
        [projections.reshape(PAIR, 2 * COEF), cosv, sinv],
        [pltpu.HBM((NG, COMB, CW), BF)],
    )

    picked, own = call(
        select_kernel,
        "select",
        [idx, x1],
        [pltpu.VMEM((NZ * 8, CW), BF), pltpu.HBM((8, 128), F32)],
        near=(1,),
        scalars=1,
        scratch=[pltpu.VMEM((2 * GR * 16, 128), F32)],
    )
    y2 = a2a(picked.reshape(NZ, 8, CW), "z").reshape(NZ * 8, CW)

    (spread,) = call(
        spread_kernel,
        "spread",
        [y2],
        [pltpu.HBM((NG, SLOTS, CW), BF)],
        near=(0,),
        away=(0,),
        scratch=[pltpu.VMEM((SLOTS, CW), BF), pltpu.SemaphoreType.DMA((NG,))],
    )
    rows = a2a(spread, ("x", "y"))
    (info,) = call(
        info_kernel,
        "info",
        [idx, y2, own],
        [pltpu.VMEM((6, NZ, 128), F32)],
        near=(1,),
        scalars=1,
    )
    table, info = lax.optimization_barrier((table, info))

    scores, lse = call(
        score_kernel,
        "score",
        [table, rows],
        [pltpu.VMEM((COMB, 128), F32), pltpu.VMEM((NC * NG, 1, 128), F32)],
        near=(1,),
        far=(0,),
        scratch=[pltpu.VMEM((NG, COMB, CW), BF), pltpu.SemaphoreType.DMA((NG,))],
    )
    l4 = a2a(lse, ("core", "x", "y"))
    (merged,) = call(
        merge_kernel, "merge", [l4], [pltpu.VMEM((NZ, NC, 128), F32)], near=(0,)
    )
    l5 = a2a(merged, "z")

    back, ev = call(
        back_kernel,
        "back",
        [l5, info, scores, rows, cosv, sinv],
        [pltpu.HBM((PAIR, 2 * COEF), BF), pltpu.HBM((1, 1), F32)],
        near=(0, 1, 2, 3),
        far=(4, 5),
        scratch=[
            pltpu.VMEM((NT, COEF), F32),
            pltpu.VMEM((NT, COEF), F32),
            pltpu.SemaphoreType.DMA((2,)),
        ],
    )
    return back.reshape(projections.shape), ev.reshape(1)


def solution(mesh):
    fine = Mesh(mesh.devices.reshape(NX, NY, NZ, NC), ("x", "y", "z", "core"))
    every = ("z", "core", "x", "y")
    cls = ("x", "y")
    pose = ("z", "core")
    return jax.shard_map(
        per_device,
        mesh=fine,
        in_specs=(P(every, None), P(every, None), P(cls, pose, None), P()),
        out_specs=(P(cls, pose, None), P(every)),
        check_vma=False,
    )
```

```python
import jax
import jax.numpy as jnp
from jax import lax
from jax.experimental import pallas as pl
from jax.experimental.pallas import tpu as pltpu
from jax.sharding import Mesh, PartitionSpec as P

BF = jnp.bfloat16
F32 = jnp.float32
I32 = jnp.int32
NEG = -3.0e38

NX, NY, NZ, NC = 4, 4, 16, 2
NG = NX * NY
GR = 16
CAP = 3
BINS = 32
NT = 4
COEF = 8192
CH = COEF // NG
CW = 2 * CH
PAIR = 32
COMB = NT * PAIR
SLOTS = 2 * GR * CAP

FIRST_Z = 8
PLANE = [((i // NY + 2) % NX) * NY + (i % NY + 2) % NY for i in range(NG)]
ALONG_Z = [[(i + FIRST_Z) % NZ for i in range(NZ)]]
IN_PLANE = [PLANE]
IN_CHIPS = [PLANE + [NG + g for g in PLANE]]


def iota(shape, dim):
    return lax.broadcasted_iota(I32, shape, dim)


def nt_dot(a, b):
    return lax.dot_general(a, b, (((1,), (1,)), ((), ())), preferred_element_type=F32)


def nn_dot(a, b):
    return lax.dot_general(a, b, (((1,), (0,)), ((), ())), preferred_element_type=F32)


def vmem():
    return pl.BlockSpec(memory_space=pltpu.VMEM)


def anywhere():
    return pl.BlockSpec(memory_space=pltpu.HBM)


def smem():
    return pl.BlockSpec(memory_space=pltpu.SMEM)


def prepare_kernel(sig_ref, x_ref, out_ref, scr):
    lane = iota((1, 128), 1)
    hit = (lane == sig_ref[0, 0]) | (lane == sig_ref[0, 1]) | (lane == sig_ref[0, 2])
    member = jnp.where(hit, 1.0, 0.0)
    scr[...] = jnp.zeros((NG * 16, 128), F32)
    scr[pl.ds(8, NG, stride=16), :] = jnp.broadcast_to(member, (NG, 128))
    x = x_ref[...].astype(F32)
    for g in range(NG):
        for j in range(CH // 128):
            at = g * CH + j * 128
            scr[g * 16 + j : g * 16 + j + 1, :] = x[:, at : at + 128]
            at = at + COEF
            scr[g * 16 + 4 + j : g * 16 + 5 + j, :] = x[:, at : at + 128]
    v = scr[...].reshape(NG, 16, 128).astype(BF)
    out_ref[:NG] = v
    out_ref[NG:] = v


def select_kernel(idx_ref, x_ref, out_ref, own_ref, scr):
    core = idx_ref[0]
    scr[...] = x_ref[...].astype(F32).reshape(2 * GR * 16, 128)
    member = scr[pl.ds(8, 2 * GR, stride=16), :]
    row = iota((32, 32), 0)
    col = iota((32, 32), 1)
    tri = jnp.where((row // GR == col // GR) & (col < row), 1.0, 0.0).astype(BF)
    rank = nn_dot(tri, member.astype(BF))
    both = (member + pltpu.roll(rank, 32, 1)).astype(BF)
    to_z = (iota((128, 128), 0) // 8 + FIRST_Z) % NZ
    pick = (iota((128, 128), 1) == 2 * to_z + core).astype(F32).astype(BF)
    mem = nt_dot(pick, member.astype(BF))
    rnk = nt_dot(pick, rank.astype(BF)).astype(I32)
    k = iota((128, 32), 0) % 8
    block = iota((128, 32), 1) // GR
    rnk = jnp.where(mem > 0.5, rnk + CAP * block, -1)
    rank_ok = (rnk >= CAP * block) & (rnk < CAP * block + CAP)
    rnk = jnp.where(rank_ok, rnk, -1)
    sel = jnp.where(rnk == k, 1.0, 0.0).astype(BF)
    for j in range(8):
        rows = scr[pl.ds(j, 2 * GR, stride=16), :].astype(BF)
        o = nn_dot(sel, rows)
        if j < 6:
            sel6 = jnp.where((k == 6) & (rnk == j), 1.0, 0.0).astype(BF)
            o = o + nn_dot(sel6, both)
        out_ref[:, j * 128 : (j + 1) * 128] = o.astype(BF)
    mine = iota((32, 128), 0) == core * GR + idx_ref[2]
    own = jnp.sum(jnp.where(mine, both.astype(F32), 0.0), axis=0, keepdims=True)
    own_ref[...] = jnp.broadcast_to(own, (8, 128))


def spread_kernel(y_ref, out_ref, scr, sem):
    s = iota((SLOTS, 128), 0)
    compact = jnp.where(iota((SLOTS, 128), 1) == (s // 6) * 8 + s % 6, 1.0, 0.0).astype(BF)
    scr[...] = nn_dot(compact, y_ref[...]).astype(BF)
    copies = [pltpu.make_async_copy(scr, out_ref.at[g], sem.at[g]) for g in range(NG)]
    for c in copies:
        c.start()
    for c in copies:
        c.wait()


def info_kernel(idx_ref, y_ref, own_ref, out_ref):
    s = iota((128, 128), 0)
    info = jnp.zeros((128, 128), F32)
    for j in range(6):
        hit = (iota((128, 128), 1) == (s // 6) * 8 + 6) & (s % 6 == j) & (s < SLOTS)
        info = info + nn_dot(
            jnp.where(hit, 1.0, 0.0).astype(BF), y_ref[:, j * 128 : (j + 1) * 128]
        )
    info = info.astype(BF)
    own = own_ref[...].astype(BF)
    z = (iota((16, 128), 0) + FIRST_Z) % NZ
    lane = iota((16, 128), 1)
    for c in range(2):
        pm = jnp.where(lane == 2 * z + c, 1.0, 0.0).astype(BF)
        pr = jnp.where(lane == 32 + 2 * z + c, 1.0, 0.0).astype(BF)
        out_ref[c] = nt_dot(pm, info)
        out_ref[2 + c] = nt_dot(pr, info)
        om = nt_dot(pm, own)[:, :1]
        orank = nt_dot(pr, own)[:, :1].astype(I32)
        out_ref[4 + c] = jnp.where((om > 0.5) & (lane == CAP * idx_ref[1] + orank), 1.0, 0.0)


def rotate_kernel(p_ref, c_ref, s_ref, out_ref):
    for g in range(NG):
        lo = g * CH
        pr = p_ref[:, lo : lo + CH].astype(F32)
        pi = p_ref[:, COEF + lo : COEF + lo + CH].astype(F32)
        for t in range(NT):
            c = c_ref[t : t + 1, lo : lo + CH]
            s = s_ref[t : t + 1, lo : lo + CH]
            out_ref[g, t * PAIR : (t + 1) * PAIR, :CH] = (c * pr - s * pi).astype(BF)
            out_ref[g, t * PAIR : (t + 1) * PAIR, CH:] = (s * pr + c * pi).astype(BF)


def score_kernel(t_ref, r_ref, score_ref, lse_ref, scr, sem):
    copies = [pltpu.make_async_copy(t_ref.at[g], scr.at[g], sem.at[g]) for g in range(NG)]
    for c in copies:
        c.start()
    acc = jnp.zeros((COMB, SLOTS), F32)
    for g in range(NG):
        copies[g].wait()
        acc = acc + nt_dot(scr[g], r_ref[g])
    score_ref[...] = jnp.zeros((COMB, 128), F32)
    score_ref[:, :SLOTS] = acc
    sc = score_ref[...]
    top = jnp.max(sc, axis=0, keepdims=True)
    lse = top + jnp.log(jnp.sum(jnp.exp(sc - top), axis=0, keepdims=True))
    lse_ref[...] = jnp.broadcast_to(lse[None], (NC * NG, 1, 128))


def merge_kernel(l_ref, out_ref):
    parts = []
    for c in range(NC):
        v = l_ref[c * NG : (c + 1) * NG].reshape(NG, 128)
        top = jnp.max(v, axis=0, keepdims=True)
        parts.append(top + jnp.log(jnp.sum(jnp.exp(v - top), axis=0, keepdims=True)))
    both = jnp.concatenate(parts, axis=0)
    out_ref[...] = jnp.broadcast_to(both[None], (NZ, NC, 128))


def back_kernel(
    l_ref, info_ref, score_ref, r_ref, cos_ref, sin_ref, out_ref, ev_ref, c_ref, s_ref, sem
):
    copies = [
        pltpu.make_async_copy(cos_ref, c_ref, sem.at[0]),
        pltpu.make_async_copy(sin_ref, s_ref, sem.at[1]),
    ]
    for c in copies:
        c.start()
    lane3 = iota((NZ, 128), 1) % CAP
    sel, own = [], []
    for c in range(NC):
        level = l_ref[:, c, :]
        shift = info_ref[2 + c].astype(I32) - lane3
        v = level
        for d in (-2, -1, 1, 2):
            v = jnp.where(shift == d, pltpu.roll(level, (-d) % 128, 1), v)
        sel.append((info_ref[c] > 0.5, v))
        own.append((info_ref[4 + c] > 0.5, level))

    def lse(pair, axes):
        a, b = (jnp.where(m, v, NEG) for m, v in pair)
        top = jnp.max(jnp.maximum(a, b), axis=axes, keepdims=True)
        tot = sum(jnp.where(m, jnp.exp(v - top), 0.0) for m, v in pair)
        return top, jnp.sum(tot, axis=axes, keepdims=True)

    top, tot = lse(own, (0, 1))
    ev_ref[...] = top + jnp.log(tot)
    top, tot = lse(sel, (0,))
    level = jnp.where(tot > 0.0, top + jnp.log(jnp.where(tot > 0.0, tot, 1.0)), 0.0)
    w = jnp.exp(score_ref[...] - level)[:, :SLOTS].astype(BF)
    for c in copies:
        c.wait()
    for g in range(NG):
        part = nn_dot(w, r_ref[g])
        re = jnp.zeros((PAIR, CH), F32)
        im = jnp.zeros((PAIR, CH), F32)
        for t in range(NT):
            c = c_ref[t : t + 1, g * CH : (g + 1) * CH]
            s = s_ref[t : t + 1, g * CH : (g + 1) * CH]
            gr = part[t * PAIR : (t + 1) * PAIR, :CH]
            gi = part[t * PAIR : (t + 1) * PAIR, CH:]
            re = re + (c * gr + s * gi)
            im = im + (c * gi - s * gr)
        out_ref[:, g * CH : (g + 1) * CH] = re.astype(BF)
        out_ref[:, COEF + g * CH : COEF + (g + 1) * CH] = im.astype(BF)


def a2a(v, axes, order):
    return lax.all_to_all(
        v, axes, split_axis=0, concat_axis=0, tiled=True, axis_index_groups=order
    )


def call(kernel, name, operands, outs, near=(), far=(), away=(), scalars=0, scratch=()):
    operands = [
        pltpu.with_memory_space_constraint(v, pltpu.VMEM if n in near else pltpu.HBM)
        if n in near or n in far
        else v
        for n, v in enumerate(operands)
    ]
    return pl.pallas_call(
        kernel,
        in_specs=[
            smem() if n < scalars else anywhere() if n in far else vmem()
            for n in range(len(operands))
        ],
        out_specs=[anywhere() if n in away else vmem() for n in range(len(outs))],
        out_shape=list(outs),
        scratch_shapes=scratch,
        compiler_params=pltpu.CompilerParams(vmem_limit_bytes=16 << 20),
        name=name,
    )(*operands)


def per_device(images, significant, projections, phase):
    core = lax.axis_index("core")
    z = lax.axis_index("z")
    block = 2 * ((z - FIRST_Z) % NZ) + core
    x, y = lax.axis_index("x"), lax.axis_index("y")
    place = ((x + 2) % NX) * NY + (y + 2) % NY
    idx = jnp.stack([core, block, place]).astype(I32)

    (first,) = call(
        prepare_kernel,
        "prepare",
        [significant, images],
        [pltpu.VMEM((NC * NG, 16, 128), BF)],
        scalars=1,
        scratch=[pltpu.VMEM((NG * 16, 128), F32)],
    )
    x1 = a2a(first, ("core", "x", "y"), IN_CHIPS)

    cosv = jnp.cos(phase)
    sinv = jnp.sin(phase)
    (table,) = call(
        rotate_kernel,
        "rotate",
        [projections.reshape(PAIR, 2 * COEF), cosv, sinv],
        [pltpu.HBM((NG, COMB, CW), BF)],
    )

    picked, own = call(
        select_kernel,
        "select",
        [idx, x1],
        [pltpu.VMEM((NZ * 8, CW), BF), pltpu.HBM((8, 128), F32)],
        near=(1,),
        scalars=1,
        scratch=[pltpu.VMEM((2 * GR * 16, 128), F32)],
    )
    y2 = a2a(picked.reshape(NZ, 8, CW), "z", ALONG_Z).reshape(NZ * 8, CW)

    (spread,) = call(
        spread_kernel,
        "spread",
        [y2],
        [pltpu.HBM((NG, SLOTS, CW), BF)],
        near=(0,),
        away=(0,),
        scratch=[pltpu.VMEM((SLOTS, CW), BF), pltpu.SemaphoreType.DMA((NG,))],
    )
    rows = a2a(spread, ("x", "y"), IN_PLANE)
    (info,) = call(
        info_kernel,
        "info",
        [idx, y2, own],
        [pltpu.VMEM((6, NZ, 128), F32)],
        near=(1,),
        scalars=1,
    )
    table, info = lax.optimization_barrier((table, info))

    scores, lse = call(
        score_kernel,
        "score",
        [table, rows],
        [pltpu.VMEM((COMB, 128), F32), pltpu.VMEM((NC * NG, 1, 128), F32)],
        near=(1,),
        far=(0,),
        scratch=[pltpu.VMEM((NG, COMB, CW), BF), pltpu.SemaphoreType.DMA((NG,))],
    )
    l4 = a2a(lse, ("core", "x", "y"), IN_CHIPS)
    (merged,) = call(
        merge_kernel, "merge", [l4], [pltpu.VMEM((NZ, NC, 128), F32)], near=(0,)
    )
    l5 = a2a(merged, "z", ALONG_Z)

    back, ev = call(
        back_kernel,
        "back",
        [l5, info, scores, rows, cosv, sinv],
        [pltpu.HBM((PAIR, 2 * COEF), BF), pltpu.HBM((1, 1), F32)],
        near=(0, 1, 2, 3),
        far=(4, 5),
        scratch=[
            pltpu.VMEM((NT, COEF), F32),
            pltpu.VMEM((NT, COEF), F32),
            pltpu.SemaphoreType.DMA((2,)),
        ],
    )
    return back.reshape(projections.shape), ev.reshape(1)


def solution(mesh):
    fine = Mesh(mesh.devices.reshape(NX, NY, NZ, NC), ("x", "y", "z", "core"))
    every = ("z", "core", "x", "y")
    cls = ("x", "y")
    pose = ("z", "core")
    return jax.shard_map(
        per_device,
        mesh=fine,
        in_specs=(P(every, None), P(every, None), P(cls, pose, None), P()),
        out_specs=(P(cls, pose, None), P(every)),
        check_vma=False,
    )
```

```python
import jax
import jax.numpy as jnp
from jax import lax
from jax.experimental import pallas as pl
from jax.experimental.pallas import tpu as pltpu
from jax.sharding import Mesh, PartitionSpec as P

BF = jnp.bfloat16
F32 = jnp.float32
I32 = jnp.int32
NEG = -3.0e38

NX, NY, NZ, NC = 4, 4, 16, 2
NG = NX * NY
GR = 16
CAP = 3
BINS = 32
NT = 4
COEF = 8192
CH = COEF // NG
CW = 2 * CH
PAIR = 32
COMB = NT * PAIR
SLOTS = 2 * GR * CAP

FIRST_Z = 8
TURN = [2, 3, 0, 1]
PLANES = [
    [x * NY + y for y in TURN for x in TURN],
    [x * NY + y for x in TURN for y in TURN],
]
ALONG_Z = [[(i + FIRST_Z) % NZ for i in range(NZ)]]
IN_CHIPS = [PLANES[0] + [NG + g for g in PLANES[1]]]
LINES = (
    [[x * NY + y for x in TURN] for y in range(NY)],
    [[x * NY + y for y in TURN] for x in range(NX)],
)
STAGES = [
    LINES[c] + [[NG + g for g in line] for line in LINES[1 - c]] for c in range(2)
]
AHEAD = 16


def iota(shape, dim):
    return lax.broadcasted_iota(I32, shape, dim)


def nt_dot(a, b):
    return lax.dot_general(a, b, (((1,), (1,)), ((), ())), preferred_element_type=F32)


def nn_dot(a, b):
    return lax.dot_general(a, b, (((1,), (0,)), ((), ())), preferred_element_type=F32)


def vmem():
    return pl.BlockSpec(memory_space=pltpu.VMEM)


def anywhere():
    return pl.BlockSpec(memory_space=pltpu.HBM)


def smem():
    return pl.BlockSpec(memory_space=pltpu.SMEM)


def prepare_kernel(sig_hbm, x_hbm, out_ref, sig_ref, x_ref, scr, sem):
    copies = [
        pltpu.make_async_copy(sig_hbm, sig_ref, sem.at[0]),
        pltpu.make_async_copy(x_hbm, x_ref, sem.at[1]),
    ]
    for c in copies:
        c.start()
    scr[...] = jnp.zeros((NG * 16, 128), F32)
    for c in copies:
        c.wait()
    lane = iota((1, 128), 1)
    hit = (lane == sig_ref[0, 0]) | (lane == sig_ref[0, 1]) | (lane == sig_ref[0, 2])
    member = jnp.where(hit, 1.0, 0.0)
    scr[pl.ds(8, NG, stride=16), :] = jnp.broadcast_to(member, (NG, 128))
    x = x_ref[...].astype(F32)
    for g in range(NG):
        for j in range(CH // 128):
            at = g * CH + j * 128
            scr[g * 16 + j : g * 16 + j + 1, :] = x[:, at : at + 128]
            at = at + COEF
            scr[g * 16 + 4 + j : g * 16 + 5 + j, :] = x[:, at : at + 128]
    v = scr[...].reshape(NG, 16, 128).astype(BF)
    out_ref[:NG] = v
    out_ref[NG:] = v


def select_kernel(idx_ref, x_ref, out_ref, own_ref, scr):
    core = idx_ref[0]
    scr[...] = x_ref[...].astype(F32).reshape(2 * GR * 16, 128)
    member = scr[pl.ds(8, 2 * GR, stride=16), :]
    row = iota((32, 32), 0)
    col = iota((32, 32), 1)
    tri = jnp.where((row // GR == col // GR) & (col < row), 1.0, 0.0).astype(BF)
    rank = nn_dot(tri, member.astype(BF))
    both = (member + pltpu.roll(rank, 32, 1)).astype(BF)
    to_z = (iota((128, 128), 0) // 8 + FIRST_Z) % NZ
    pick = (iota((128, 128), 1) == 2 * to_z + core).astype(F32).astype(BF)
    mem = nt_dot(pick, member.astype(BF))
    rnk = nt_dot(pick, rank.astype(BF)).astype(I32)
    k = iota((128, 32), 0) % 8
    block = iota((128, 32), 1) // GR
    rnk = jnp.where(mem > 0.5, rnk + CAP * block, -1)
    rank_ok = (rnk >= CAP * block) & (rnk < CAP * block + CAP)
    rnk = jnp.where(rank_ok, rnk, -1)
    sel = jnp.where(rnk == k, 1.0, 0.0).astype(BF)
    for j in range(8):
        rows = scr[pl.ds(j, 2 * GR, stride=16), :].astype(BF)
        o = nn_dot(sel, rows)
        if j < 6:
            sel6 = jnp.where((k == 6) & (rnk == j), 1.0, 0.0).astype(BF)
            o = o + nn_dot(sel6, both)
        out_ref[:, j * 128 : (j + 1) * 128] = o.astype(BF)
    mine = iota((32, 128), 0) == core * GR + idx_ref[2]
    own = jnp.sum(jnp.where(mine, both.astype(F32), 0.0), axis=0, keepdims=True)
    own_ref[...] = jnp.broadcast_to(own, (8, 128))


def spread_kernel(y_ref, out_ref, scr, sem):
    s = iota((SLOTS, 128), 0)
    compact = jnp.where(iota((SLOTS, 128), 1) == (s // 6) * 8 + s % 6, 1.0, 0.0).astype(BF)
    scr[...] = nn_dot(compact, y_ref[...]).astype(BF)
    copies = [pltpu.make_async_copy(scr, out_ref.at[g], sem.at[g]) for g in range(NX)]
    for c in copies:
        c.start()
    for c in copies:
        c.wait()


def repeat_kernel(y_ref, out_ref, sem):
    copies = [pltpu.make_async_copy(y_ref, out_ref.at[g], sem.at[g]) for g in range(NX)]
    for c in copies:
        c.start()
    for c in copies:
        c.wait()


def info_kernel(idx_ref, y_ref, own_ref, out_ref):
    s = iota((128, 128), 0)
    info = jnp.zeros((128, 128), F32)
    for j in range(6):
        hit = (iota((128, 128), 1) == (s // 6) * 8 + 6) & (s % 6 == j) & (s < SLOTS)
        info = info + nn_dot(
            jnp.where(hit, 1.0, 0.0).astype(BF), y_ref[:, j * 128 : (j + 1) * 128]
        )
    info = info.astype(BF)
    own = own_ref[...].astype(BF)
    z = (iota((16, 128), 0) + FIRST_Z) % NZ
    lane = iota((16, 128), 1)
    for c in range(2):
        pm = jnp.where(lane == 2 * z + c, 1.0, 0.0).astype(BF)
        pr = jnp.where(lane == 32 + 2 * z + c, 1.0, 0.0).astype(BF)
        out_ref[c] = nt_dot(pm, info)
        out_ref[2 + c] = nt_dot(pr, info)
        om = nt_dot(pm, own)[:, :1]
        orank = nt_dot(pr, own)[:, :1].astype(I32)
        out_ref[4 + c] = jnp.where((om > 0.5) & (lane == CAP * idx_ref[1] + orank), 1.0, 0.0)


def rotate_kernel(p_ref, c_ref, s_ref, out_ref):
    for g in range(NG):
        lo = g * CH
        pr = p_ref[:, lo : lo + CH].astype(F32)
        pi = p_ref[:, COEF + lo : COEF + lo + CH].astype(F32)
        for t in range(NT):
            c = c_ref[t : t + 1, lo : lo + CH]
            s = s_ref[t : t + 1, lo : lo + CH]
            out_ref[g, t * PAIR : (t + 1) * PAIR, :CH] = (c * pr - s * pi).astype(BF)
            out_ref[g, t * PAIR : (t + 1) * PAIR, CH:] = (s * pr + c * pi).astype(BF)


def score_kernel(t_ref, r_ref, score_ref, lse_ref, scr, sem):
    copies = [pltpu.make_async_copy(t_ref.at[g], scr.at[g], sem.at[g]) for g in range(NG)]
    for g in range(AHEAD):
        copies[g].start()
    acc = jnp.zeros((COMB, SLOTS), F32)
    for g in range(NG):
        copies[g].wait()
        if g + AHEAD < NG:
            copies[g + AHEAD].start()
        acc = acc + nt_dot(scr[g], r_ref[g])
    score_ref[...] = jnp.zeros((COMB, 128), F32)
    score_ref[:, :SLOTS] = acc
    sc = score_ref[...]
    top = jnp.max(sc, axis=0, keepdims=True)
    lse = top + jnp.log(jnp.sum(jnp.exp(sc - top), axis=0, keepdims=True))
    lse_ref[...] = jnp.broadcast_to(lse[None], (NC * NG, 1, 128))


def merge_kernel(l_ref, out_ref):
    parts = []
    for c in range(NC):
        v = l_ref[c * NG : (c + 1) * NG].reshape(NG, 128)
        top = jnp.max(v, axis=0, keepdims=True)
        parts.append(top + jnp.log(jnp.sum(jnp.exp(v - top), axis=0, keepdims=True)))
    both = jnp.concatenate(parts, axis=0)
    out_ref[...] = jnp.broadcast_to(both[None], (NZ, NC, 128))


def back_kernel(
    l_ref, info_ref, score_ref, r_ref, cos_ref, sin_ref, out_ref, ev_ref, c_ref, s_ref, sem
):
    copies = [
        pltpu.make_async_copy(cos_ref, c_ref, sem.at[0]),
        pltpu.make_async_copy(sin_ref, s_ref, sem.at[1]),
    ]
    for c in copies:
        c.start()
    lane3 = iota((NZ, 128), 1) % CAP
    sel, own = [], []
    for c in range(NC):
        level = l_ref[:, c, :]
        shift = info_ref[2 + c].astype(I32) - lane3
        v = level
        for d in (-2, -1, 1, 2):
            v = jnp.where(shift == d, pltpu.roll(level, (-d) % 128, 1), v)
        sel.append((info_ref[c] > 0.5, v))
        own.append((info_ref[4 + c] > 0.5, level))

    def lse(pair, axes):
        a, b = (jnp.where(m, v, NEG) for m, v in pair)
        top = jnp.max(jnp.maximum(a, b), axis=axes, keepdims=True)
        tot = sum(jnp.where(m, jnp.exp(v - top), 0.0) for m, v in pair)
        return top, jnp.sum(tot, axis=axes, keepdims=True)

    top, tot = lse(own, (0, 1))
    ev_ref[...] = top + jnp.log(tot)
    top, tot = lse(sel, (0,))
    level = jnp.where(tot > 0.0, top + jnp.log(jnp.where(tot > 0.0, tot, 1.0)), 0.0)
    w = jnp.exp(score_ref[...] - level)[:, :SLOTS].astype(BF)
    for c in copies:
        c.wait()
    for g in range(NG):
        part = nn_dot(w, r_ref[g])
        re = jnp.zeros((PAIR, CH), F32)
        im = jnp.zeros((PAIR, CH), F32)
        for t in range(NT):
            c = c_ref[t : t + 1, g * CH : (g + 1) * CH]
            s = s_ref[t : t + 1, g * CH : (g + 1) * CH]
            gr = part[t * PAIR : (t + 1) * PAIR, :CH]
            gi = part[t * PAIR : (t + 1) * PAIR, CH:]
            re = re + (c * gr + s * gi)
            im = im + (c * gi - s * gr)
        out_ref[:, g * CH : (g + 1) * CH] = re.astype(BF)
        out_ref[:, COEF + g * CH : COEF + (g + 1) * CH] = im.astype(BF)


def a2a(v, axes, order):
    return lax.all_to_all(
        v, axes, split_axis=0, concat_axis=0, tiled=True, axis_index_groups=order
    )


def call(kernel, name, operands, outs, near=(), far=(), away=(), scalars=0, scratch=()):
    operands = [
        pltpu.with_memory_space_constraint(v, pltpu.VMEM if n in near else pltpu.HBM)
        if n in near or n in far
        else v
        for n, v in enumerate(operands)
    ]
    return pl.pallas_call(
        kernel,
        in_specs=[
            smem() if n < scalars else anywhere() if n in far else vmem()
            for n in range(len(operands))
        ],
        out_specs=[anywhere() if n in away else vmem() for n in range(len(outs))],
        out_shape=list(outs),
        scratch_shapes=scratch,
        compiler_params=pltpu.CompilerParams(vmem_limit_bytes=16 << 20),
        name=name,
    )(*operands)


def per_device(images, significant, projections, phase):
    core = lax.axis_index("core")
    z = lax.axis_index("z")
    block = 2 * ((z - FIRST_Z) % NZ) + core
    x, y = (lax.axis_index("x") + 2) % NX, (lax.axis_index("y") + 2) % NY
    place = jnp.where(core == 0, y * NX + x, x * NY + y)
    idx = jnp.stack([core, block, place]).astype(I32)

    (first,) = call(
        prepare_kernel,
        "prepare",
        [significant, images],
        [pltpu.HBM((NC * NG, 16, 128), BF)],
        far=(0, 1),
        scratch=[
            pltpu.SMEM((1, 3), I32),
            pltpu.VMEM((1, 2 * COEF), BF),
            pltpu.VMEM((NG * 16, 128), F32),
            pltpu.SemaphoreType.DMA((2,)),
        ],
    )
    x1 = a2a(first, ("core", "x", "y"), IN_CHIPS)

    cosv = jnp.cos(phase)
    sinv = jnp.sin(phase)
    (table,) = call(
        rotate_kernel,
        "rotate",
        [projections.reshape(PAIR, 2 * COEF), cosv, sinv],
        [pltpu.HBM((NG, COMB, CW), BF)],
    )

    picked, own = call(
        select_kernel,
        "select",
        [idx, x1],
        [pltpu.VMEM((NZ * 8, CW), BF), pltpu.HBM((8, 128), F32)],
        near=(1,),
        scalars=1,
        scratch=[pltpu.VMEM((2 * GR * 16, 128), F32)],
    )
    y2 = a2a(picked.reshape(NZ, 8, CW), "z", ALONG_Z).reshape(NZ * 8, CW)

    (spread,) = call(
        spread_kernel,
        "spread",
        [y2],
        [pltpu.HBM((NX, SLOTS, CW), BF)],
        near=(0,),
        away=(0,),
        scratch=[pltpu.VMEM((SLOTS, CW), BF), pltpu.SemaphoreType.DMA((NX,))],
    )
    line = a2a(spread, ("core", "x", "y"), STAGES[0])
    (lines,) = call(
        repeat_kernel,
        "repeat",
        [line],
        [pltpu.HBM((NX, NX, SLOTS, CW), BF)],
        near=(0,),
        away=(0,),
        scratch=[pltpu.SemaphoreType.DMA((NX,))],
    )
    rows = a2a(lines, ("core", "x", "y"), STAGES[1]).reshape(NG, SLOTS, CW)
    (info,) = call(
        info_kernel,
        "info",
        [idx, y2, own],
        [pltpu.VMEM((6, NZ, 128), F32)],
        near=(1,),
        scalars=1,
    )
    table, info = lax.optimization_barrier((table, info))

    scores, lse = call(
        score_kernel,
        "score",
        [table, rows],
        [pltpu.VMEM((COMB, 128), F32), pltpu.VMEM((NC * NG, 1, 128), F32)],
        near=(1,),
        far=(0,),
        scratch=[pltpu.VMEM((NG, COMB, CW), BF), pltpu.SemaphoreType.DMA((NG,))],
    )
    l4 = a2a(lse, ("core", "x", "y"), IN_CHIPS)
    (merged,) = call(
        merge_kernel, "merge", [l4], [pltpu.VMEM((NZ, NC, 128), F32)], near=(0,)
    )
    l5 = a2a(merged, "z", ALONG_Z)

    back, ev = call(
        back_kernel,
        "back",
        [l5, info, scores, rows, cosv, sinv],
        [pltpu.HBM((PAIR, 2 * COEF), BF), pltpu.HBM((1, 1), F32)],
        near=(0, 1, 2, 3),
        far=(4, 5),
        scratch=[
            pltpu.VMEM((NT, COEF), F32),
            pltpu.VMEM((NT, COEF), F32),
            pltpu.SemaphoreType.DMA((2,)),
        ],
    )
    return back.reshape(projections.shape), ev.reshape(1)


def solution(mesh):
    fine = Mesh(mesh.devices.reshape(NX, NY, NZ, NC), ("x", "y", "z", "core"))
    every = ("z", "core", "x", "y")
    cls = ("x", "y")
    pose = ("z", "core")
    return jax.shard_map(
        per_device,
        mesh=fine,
        in_specs=(P(every, None), P(every, None), P(cls, pose, None), P()),
        out_specs=(P(cls, pose, None), P(every)),
        check_vma=False,
    )
```
